32 devices in a mesh: row: 4 (over z), col: 8 (over y, x, core).
Axes of the slice: x: 2, y: 2, z: 4, core: 2. Of those that a mesh axis runs over, the one named last changes fastest.
Arguments:
- trailing: float32 [16384, 3072], P('row', 'col'), may hold values from -6 to 6
- leaf_vectors: float32 [16384, 256], P(('row', 'col')), may hold values from -1 to 1, as said below
- leaf_factor: float32 [1024, 256], P(('row', 'col')), may hold values from -1 to 2, as said below
- tree_vectors: float32 [1024, 256], P(('row', 'col')), may hold values from -1 to 1, as said below
- tree_factor: float32 [1024, 256], P(('row', 'col')), may hold values from -1 to 2, as said below
Outputs:
- updated: float32 [16384, 3072], P('row', 'col')
The draws below stay inside these ranges and needn't reach their ends.
Inputs may be any that keep to these rules, and one draw needn't show every extreme that they name: `leaf_vectors`: in each row block of 4096 rows, row r < 256 of the block holds 1 in column r and 0 in every column after r. `leaf_factor`: each 256 x 256 block is upper triangular with its diagonal between 1 and 2. `tree_vectors`: each 256 x 256 block is upper triangular. `tree_factor`: each 256 x 256 block is upper triangular with its diagonal between 1 and 2.
All inputs are finite; a program needn't handle non-finite values.
Results may differ from the reference program's by a relative error of at most 0.0002.
Values sent between devices are 32-bit elements; how exact they have to be, the bound alone decides.
No kernel may reach another device: no remote copies, remote signals or barrier semaphores. Data moves between devices by JAX's collectives and lax.ppermute only.
A program may use at most 128 MiB of HBM per device.

```python
import math
import jax
import jax.numpy as jnp
from jax import lax

B = 256
R_DEV = 4096
M = 16384
N = 3072


def draw_leaf_vectors(key, part):
    sampled = jax.random.truncated_normal(jax.random.fold_in(key, 11), -6.0, 6.0, (M, B), jnp.float32) * (1.0 / math.sqrt(R_DEV))
    row_in_block = (jnp.arange(M) % R_DEV)[:, None]
    column_ids = jnp.arange(B)[None, :]
    return jnp.where(column_ids < row_in_block, sampled, jnp.where(column_ids == row_in_block, 1.0, 0.0)).astype(jnp.float32)


def triangular_factor(key, salt):
    count = M // R_DEV * B
    folded = jax.random.fold_in(key, salt)
    diagonal_values = jax.random.uniform(jax.random.fold_in(folded, 1), (count, B), jnp.float32, 1.0, 2.0)
    sampled = jax.random.truncated_normal(jax.random.fold_in(folded, 2), -4.0, 4.0, (count, B), jnp.float32) * (0.5 / math.sqrt(B))
    row_in_block = (jnp.arange(count) % B)[:, None]
    column_ids = jnp.arange(B)[None, :]
    return jnp.where(column_ids > row_in_block, sampled, jnp.where(column_ids == row_in_block, diagonal_values, 0.0)).astype(jnp.float32)


def draw_leaf_factor(key, part):
    return triangular_factor(key, 21)


def draw_tree_factor(key, part):
    return triangular_factor(key, 23)


def draw_tree_vectors(key, part):
    count = M // R_DEV * B
    sampled = jax.random.truncated_normal(jax.random.fold_in(key, 31), -4.0, 4.0, (count, B), jnp.float32) * (1.0 / math.sqrt(B))
    row_in_block = (jnp.arange(count) % B)[:, None]
    column_ids = jnp.arange(B)[None, :]
    return jnp.where(column_ids >= row_in_block, sampled, 0.0).astype(jnp.float32)


def shard_levels(stream_key, dims, shards, low, largest):
    gain = 1.0
    for position, shards_of in shards:
        steps = jax.random.uniform(jax.random.fold_in(jax.random.fold_in(stream_key, 6), position), (shards_of,), jnp.float32, low / len(shards), largest / len(shards))
        gain = gain * jnp.repeat(jnp.exp(steps), dims[position] // shards_of).reshape((-1,) + (1,) * (len(dims) - 1 - position))
    return gain


def gaussian(stream_key, extent, scale, most, split=(), held_as=jnp.bfloat16):
    result = scale * jax.random.normal(stream_key, extent, jnp.float32)
    if split:
        result = result * shard_levels(stream_key, extent, split, -0.22, 0.18)
    return jnp.clip(result, -most, most).astype(held_as)


def setup_inputs(seed: int = 0) -> dict:
    key_of = jax.random.split(jax.random.key(seed), 6)
    trailing = gaussian(key_of[0], (M, N), 1.0, 6.0, ((0, 4), (1, 8)), jnp.float32)
    leaf_vectors = draw_leaf_vectors(jax.random.fold_in(key_of[5], 71), 0)
    leaf_factor = draw_leaf_factor(jax.random.fold_in(key_of[5], 71), 0)
    tree_vectors = draw_tree_vectors(jax.random.fold_in(key_of[5], 71), 0)
    tree_factor = draw_tree_factor(jax.random.fold_in(key_of[5], 71), 0)
    return dict(trailing=trailing, leaf_vectors=leaf_vectors, leaf_factor=leaf_factor, tree_vectors=tree_vectors, tree_factor=tree_factor)


highest = lax.Precision.HIGHEST
contract_rows = (((0,), (0,)), ((), ()))


def left_product(first, second):
    return lax.dot_general(first, second, contract_rows, precision=highest, preferred_element_type=jnp.float32)


def plain_product(first, second):
    return jnp.dot(first, second, precision=highest, preferred_element_type=jnp.float32)


def apply_leaf(operands):
    row_block, vectors, factor = operands
    weights = left_product(factor, left_product(vectors, row_block))
    return row_block - plain_product(vectors, weights)


def reference(trailing, leaf_vectors, leaf_factor, tree_vectors, tree_factor):
    blocks_count = trailing.shape[0] // R_DEV
    blocks = trailing.reshape(blocks_count, R_DEV, trailing.shape[1])
    updated = lax.map(apply_leaf, (blocks, leaf_vectors.reshape(blocks_count, R_DEV, B), leaf_factor.reshape(blocks_count, B, B)))
    top_rows = [updated[block_index, :B, :] for block_index in range(blocks_count)]
    stride = 1
    while stride < blocks_count:
        for leader in range(0, blocks_count, 2 * stride):
            partner = leader + stride
            vectors = tree_vectors[partner * B:(partner + 1) * B]
            factor = tree_factor[partner * B:(partner + 1) * B]
            weights = left_product(factor, top_rows[leader] + left_product(vectors, top_rows[partner]))
            top_rows[leader] = top_rows[leader] - weights
            top_rows[partner] = top_rows[partner] - plain_product(vectors, weights)
        stride = stride * 2
    return updated.at[:, :B, :].set(jnp.stack(top_rows)).reshape(trailing.shape)
```

```python
import functools

import jax
import jax.numpy as jnp
from jax import lax
from jax.experimental import pallas as pl
from jax.experimental.pallas import tpu as pltpu
from jax.sharding import PartitionSpec as P


ROWS = (((0,), (0,)), ((), ()))
PLAIN = (((1,), (0,)), ((), ()))
ANY = pl.BlockSpec(memory_space=pl.ANY)
SCALARS = pl.BlockSpec(memory_space=pltpu.SMEM)


def halves(array):
    high = array.astype(jnp.bfloat16)
    return high, (array - high.astype(jnp.float32)).astype(jnp.bfloat16)


def narrow(first, second, dims):
    return lax.dot_general(first, second, dims, preferred_element_type=jnp.float32)


def product(first, second, dims):
    first_high, first_low = halves(first)
    second_high, second_low = halves(second)
    return narrow(first_high, second_high, dims) + (
        narrow(first_high, second_low, dims) + narrow(first_low, second_high, dims)
    )


def exchanged(array, axis, mask):
    return lax.ppermute(array, axis, [(i, i ^ mask) for i in range(lax.axis_size(axis))])


def out(shape):
    return jax.ShapeDtypeStruct(shape, jnp.float32)


def gram_step(spot, pieces, trailing, held, total):
    shard = trailing.shape[0] // lax.axis_size("col")
    first = held is None
    count = len(pieces)
    width, columns = pieces[0][2].shape[1], trailing.shape[1]
    tall = max(piece[2].shape[0] for piece in pieces)

    def kernel(spot_ref, trailing_ref, *refs):
        piece_refs, refs = refs[:count], refs[count:]
        if not first:
            refs = refs[1:]
            total_in, refs = refs[0], refs[1:]
        held_ref, total_ref, rows_of, block_of, sems = refs
        loads, stores = [], []
        for n, (mask, offset, array) in enumerate(pieces):
            size = array.shape[0]
            start = pl.multiple_of((spot_ref[0] ^ mask) * shard + offset, size)
            loads.append((
                pltpu.make_async_copy(piece_refs[n], block_of.at[n, pl.ds(0, size)], sems.at[0, n]),
                pltpu.make_async_copy(trailing_ref.at[pl.ds(start, size)], rows_of.at[n, pl.ds(0, size)], sems.at[1, n]),
            ))
            stores.append(pltpu.make_async_copy(block_of.at[n, pl.ds(0, size)], held_ref.at[pl.ds(start, size)], sems.at[2, n]))
            for copy in loads[-1]:
                copy.start()
        sum_of = None if first else total_in[...]
        for n, (mask, offset, array) in enumerate(pieces):
            size = array.shape[0]
            for copy in loads[n]:
                copy.wait()
            stores[n].start()
            term = product(block_of[n, :size], rows_of[n, :size], ROWS)
            sum_of = term if sum_of is None else sum_of + term
        total_ref[...] = sum_of
        for copy in stores:
            copy.wait()

    whole = pl.BlockSpec(memory_space=pltpu.VMEM)
    arrays = [piece[2] for piece in pieces]
    flops = 6 * sum(a.shape[0] for a in arrays) * width * columns
    return pl.pallas_call(
        kernel,
        in_specs=[SCALARS, ANY] + [ANY] * count + ([] if first else [ANY, whole]),
        out_specs=[ANY, whole],
        out_shape=[out((trailing.shape[0], width)), out((width, columns))],
        scratch_shapes=[
            pltpu.VMEM((count, tall, columns), jnp.float32),
            pltpu.VMEM((count, tall, width), jnp.float32),
            pltpu.SemaphoreType.DMA((3, count)),
        ],
        input_output_aliases={} if first else {2 + count: 0},
        cost_estimate=pl.CostEstimate(flops=flops, bytes_accessed=4 * sum(a.shape[0] for a in arrays) * (columns + 2 * width), transcendentals=0),
        name="gram_step",
    )(spot, trailing, *arrays, *(() if first else (held, total)))


def gathered_square(spot_ref, source_ref, order, row, height, square):
    size = square.shape[0] // len(order)
    for n, mask in enumerate(order):
        to = pl.multiple_of((spot_ref[0] ^ mask) * size, size)
        square[pl.ds(to, size), :] = source_ref[n * height + row : n * height + row + size, :]


def weigh(spot, total, factors, order, trailing, held):
    width, columns = total.shape

    def kernel(spot_ref, total_ref, factors_ref, trailing_ref, held_ref, weights_ref, top_ref, square, rows_of, block_of, sems):
        loads = (
            pltpu.make_async_copy(held_ref.at[pl.ds(0, width)], block_of, sems.at[0]),
            pltpu.make_async_copy(trailing_ref.at[pl.ds(0, width)], rows_of, sems.at[1]),
        )
        for copy in loads:
            copy.start()
        gathered_square(spot_ref, factors_ref, order, 0, factors_ref.shape[0] // len(order), square)
        weights = product(square[...], total_ref[...], ROWS)
        weights_ref[...] = weights
        for copy in loads:
            copy.wait()
        top_ref[...] = rows_of[...] - product(block_of[...], weights, PLAIN)

    whole = pl.BlockSpec(memory_space=pltpu.VMEM)
    return pl.pallas_call(
        kernel,
        in_specs=[SCALARS, whole, whole, ANY, ANY],
        out_specs=[whole, whole],
        out_shape=[out((width, columns)), out((width, columns))],
        scratch_shapes=[
            pltpu.VMEM((width, width), jnp.float32),
            pltpu.VMEM((width, columns), jnp.float32),
            pltpu.VMEM((width, width), jnp.float32),
            pltpu.SemaphoreType.DMA((2,)),
        ],
        cost_estimate=pl.CostEstimate(flops=12 * width * width * columns, bytes_accessed=16 * width * columns, transcendentals=0),
        name="weigh",
    )(spot, total, factors, trailing, held)


def update(trailing, held, weights):
    width, columns = weights.shape
    rows = trailing.shape[0]
    tile = width

    def kernel(trailing_ref, held_ref, weights_ref, out_ref):
        out_ref[...] = trailing_ref[...] - product(held_ref[...], weights_ref[...], PLAIN)

    return pl.pallas_call(
        kernel,
        grid=(rows // tile - 1,),
        in_specs=[
            pl.BlockSpec((tile, columns), lambda i: (i + 1, 0)),
            pl.BlockSpec((tile, width), lambda i: (i + 1, 0)),
            pl.BlockSpec((width, columns), lambda i: (0, 0)),
        ],
        out_specs=pl.BlockSpec((tile, columns), lambda i: (i + 1, 0)),
        out_shape=out(trailing.shape),
        cost_estimate=pl.CostEstimate(flops=6 * rows * width * columns, bytes_accessed=4 * rows * (2 * columns + width), transcendentals=0),
        name="update",
    )(trailing, held, weights)


def combine(spot, level, current, received, pair, order, updated):
    width, columns = current.shape
    height = pair.shape[0] // len(order)
    share = width // len(order)
    last = updated is not None

    def kernel(spot_ref, current_ref, received_ref, pair_ref, *refs):
        if last:
            refs = refs[1:]
        top_ref, vectors, factor, *rest = refs
        gathered_square(spot_ref, pair_ref, order, 2 * level * share, height, vectors)
        gathered_square(spot_ref, pair_ref, order, (2 * level + 1) * share, height, factor)
        role = spot_ref[1 + level]
        result = rest[0] if last else top_ref
        if last:
            result[...] = current_ref[...]
        else:
            result[...] = current_ref[...]

        @pl.when(role == 1)
        def _():
            weights = product(factor[...], current_ref[...] + product(vectors[...], received_ref[...], ROWS), ROWS)
            result[...] = current_ref[...] - weights

        @pl.when(role == 2)
        def _():
            weights = product(factor[...], received_ref[...] + product(vectors[...], current_ref[...], ROWS), ROWS)
            result[...] = current_ref[...] - product(vectors[...], weights, PLAIN)

        if last:
            store = pltpu.make_async_copy(result, top_ref.at[pl.ds(0, width)], rest[1].at[0])
            store.start()
            store.wait()

    whole = pl.BlockSpec(memory_space=pltpu.VMEM)
    squares = [pltpu.VMEM((width, width), jnp.float32)] * 2
    return pl.pallas_call(
        kernel,
        in_specs=[SCALARS, whole, whole, whole] + ([ANY] if last else []),
        out_specs=ANY if last else whole,
        out_shape=out(updated.shape if last else (width, columns)),
        scratch_shapes=squares + ([pltpu.VMEM((width, columns), jnp.float32), pltpu.SemaphoreType.DMA((1,))] if last else []),
        input_output_aliases={4: 0} if last else {},
        cost_estimate=pl.CostEstimate(flops=18 * width * width * columns, bytes_accessed=16 * width * columns, transcendentals=0),
        name="combine",
    )(spot, current, received, pair, *((updated,) if last else ()))


def doubled(array, masks):
    order = [0]
    for mask in masks:
        array = jnp.concatenate([array, exchanged(array, "col", mask)], 0)
        order = order + [n ^ mask for n in order]
    return array, order


def shards(trailing, leaf_vectors, leaf_factor, tree_vectors, tree_factor):
    across = lax.axis_size("col")
    down = lax.axis_size("row")
    levels = down.bit_length() - 1
    bits = [1 << n for n in range(across.bit_length() - 1)]
    place = lax.axis_index("row")
    roles = []
    for level in range(levels):
        stride = 1 << level
        inside = place % (2 * stride)
        roles.append(jnp.where(inside == 0, 1, jnp.where(inside == stride, 2, 0)))
    spot = jnp.stack([lax.axis_index("col")] + roles).astype(jnp.int32)

    if len(bits) == 3:
        core, wide, high = bits
        half = leaf_vectors.shape[0] // 2
        by_wide = exchanged(leaf_vectors, "col", wide)
        by_high = exchanged(leaf_vectors, "col", high)
        by_core = exchanged(leaf_vectors, "col", core)
        steps = [[(0, 0, leaf_vectors), (core, 0, by_core)]]
        far_a = exchanged(by_wide[:half], "col", high)
        far_b = exchanged(by_high[half:], "col", wide)
        core_wide = exchanged(by_wide, "col", core)
        core_high = exchanged(by_high, "col", core)
        steps.append([(wide, 0, by_wide), (high, 0, by_high), (wide ^ core, 0, core_wide), (high ^ core, 0, core_high)])
        far = wide ^ high
        core_a = exchanged(far_a, "col", core)
        core_b = exchanged(far_b, "col", core)
        steps.append([(far, 0, far_a), (far, half, far_b), (far ^ core, 0, core_a), (far ^ core, half, core_b)])
    else:
        blocks = [(0, 0, leaf_vectors)]
        steps = [blocks]
        for bit in reversed(bits):
            steps.append([(mask ^ bit, 0, exchanged(block, "col", bit)) for mask, _, block in blocks])
            blocks = blocks + steps[-1]
    masks = bits[1:] + bits[:1]
    factors, order = doubled(leaf_factor, masks)

    pairs = []
    own = jnp.concatenate([tree_vectors, tree_factor], 0)
    for level in range(levels):
        stride = 1 << level
        sent = lax.ppermute(own, "row", [(k + stride, k) for k in range(0, down, 2 * stride)])
        pairs.append(jnp.where(roles[level] == 2, own, sent))
    pair, _ = doubled(jnp.concatenate(pairs, 0), masks)

    held = total = None
    for pieces in steps:
        held, total = gram_step(spot, pieces, trailing, held, total)
    weights, current = weigh(spot, total, factors, order, trailing, held)
    updated = update(trailing, held, weights)
    for level in range(levels):
        stride = 1 << level
        swap = [(k, k + stride) for k in range(0, down, 2 * stride)]
        received = lax.ppermute(current, "row", swap + [(b, a) for a, b in swap])
        current = combine(spot, level, current, received, pair, order, updated if level == levels - 1 else None)
    return current


def solution(mesh):
    placed = (
        P("row", "col"),
        P(("row", "col"), None),
        P(("row", "col"), None),
        P(("row", "col"), None),
        P(("row", "col"), None),
    )
    return jax.shard_map(
        shards, mesh=mesh, in_specs=placed, out_specs=P("row", "col"), check_vma=False
    )
```

```python
import math

import jax
import jax.numpy as jnp
from jax import lax
from jax.experimental import pallas as pl
from jax.experimental.pallas import tpu as pltpu
from jax.sharding import PartitionSpec as P


ROWS = (((0,), (0,)), ((), ()))
PLAIN = (((1,), (0,)), ((), ()))
HBM = pl.BlockSpec(memory_space=pltpu.HBM)
WHOLE = pl.BlockSpec(memory_space=pltpu.VMEM)
GRANT = 4 << 20
PARTS = 8
TILES = 6


def halves(array):
    high = array.astype(jnp.bfloat16)
    return high, (array - high.astype(jnp.float32)).astype(jnp.bfloat16)


def narrow(first, second, dims):
    return lax.dot_general(first, second, dims, preferred_element_type=jnp.float32)


def product(first, second, dims):
    first_high, first_low = halves(first)
    second_high, second_low = halves(second)
    return narrow(first_high, second_high, dims) + (
        narrow(first_high, second_low, dims) + narrow(first_low, second_high, dims)
    )


def thrice(high, low, factor_high, factor_low):
    return narrow(high, factor_high, PLAIN) + (narrow(high, factor_low, PLAIN) + narrow(low, factor_high, PLAIN))


def out(*shape):
    return pltpu.VMEM(shape, jnp.float32)


def outside(*shape):
    return pltpu.HBM(shape, jnp.float32)


def role_of(level):
    stride = 1 << level
    inside = lax.rem(lax.axis_index("row"), 2 * stride)
    return jnp.where(inside == 0, 1, jnp.where(inside == stride, 2, 0))


def outer(*arrays):
    return tuple(pltpu.with_memory_space_constraint(array, pltpu.HBM) for array in arrays)


def exchanged(array, mask):
    return lax.ppermute(array, "col", [(i, i ^ mask) for i in range(lax.axis_size("col"))])


def kernel_call(kernel, arguments, flops, moved, grant=GRANT, **options):
    return pl.pallas_call(
        kernel,
        compiler_params=pltpu.CompilerParams(vmem_limit_bytes=grant),
        cost_estimate=pl.CostEstimate(flops=flops, bytes_accessed=moved, transcendentals=0),
        **options,
    )(*arguments)


def pack(leaf_vectors, leaf_factor, tree_vectors, tree_factor, ranges):
    tall, short = leaf_vectors.shape[0], leaf_factor.shape[0]
    parts = len(ranges)

    def kernel(vectors_ref, factor_ref, tree_vectors_ref, tree_factor_ref, *refs):
        *part_refs, own_ref, sems = refs
        moves = [(tree_vectors_ref, own_ref.at[pl.ds(0, short)]), (tree_factor_ref, own_ref.at[pl.ds(short, short)])]
        for (start, stop), ref in zip(ranges, part_refs):
            upper = min(stop, tall) - start
            moves.append((vectors_ref.at[pl.ds(start, upper)], ref.at[pl.ds(0, upper)]))
            if stop > tall:
                moves.append((factor_ref, ref.at[pl.ds(upper, short)]))
        copies = [pltpu.make_async_copy(source, target, sems.at[n]) for n, (source, target) in enumerate(moves)]
        for copy in copies:
            copy.start()
        for copy in copies:
            copy.wait()

    width = leaf_vectors.shape[1]
    return kernel_call(
        kernel, outer(leaf_vectors, leaf_factor, tree_vectors, tree_factor), 0, 8 * tall * width,
        in_specs=[HBM] * 4, out_specs=[WHOLE] * (parts + 1),
        out_shape=[out(stop - start, width) for start, stop in ranges] + [out(2 * short, width)],
        scratch_shapes=[pltpu.SemaphoreType.DMA((parts + 3,))],
    )


def load(array):
    rows = array.shape[0] // PARTS

    def kernel(array_ref, out_ref, high_ref, low_ref, sems):
        copies = []
        for n in range(PARTS):
            part = pl.ds(n * rows, rows)
            copies.append(pltpu.make_async_copy(array_ref.at[part], out_ref.at[part], sems.at[n]))
            copies[-1].start()
        for n, copy in enumerate(copies):
            copy.wait()
            part = pl.ds(n * rows, rows)
            high_ref[part, :], low_ref[part, :] = halves(out_ref[part, :])

    shape = array.shape
    return kernel_call(
        kernel, outer(array), 0, 12 * array.size,
        in_specs=[HBM], out_specs=[WHOLE] * 3,
        out_shape=[out(*shape), pltpu.VMEM(shape, jnp.bfloat16), pltpu.VMEM(shape, jnp.bfloat16)],
        scratch_shapes=[pltpu.SemaphoreType.DMA((PARTS,))],
    )


def join(arrays):
    def kernel(*refs):
        start = 0
        for ref in refs[:-1]:
            refs[-1][start : start + ref.shape[0], :] = ref[...]
            start += ref.shape[0]

    rows = sum(array.shape[0] for array in arrays)
    return kernel_call(
        kernel, arrays, 0, 8 * rows * arrays[0].shape[1],
        in_specs=[WHOLE] * len(arrays), out_specs=WHOLE, out_shape=out(rows, arrays[0].shape[1]),
    )


def pick(level, own, sent):
    def kernel(own_ref, sent_ref, out_ref):
        out_ref[...] = jnp.where(role_of(level) == 2, own_ref[...], sent_ref[...])

    return kernel_call(
        kernel, (own, sent), 0, 12 * own.size,
        in_specs=[WHOLE, WHOLE], out_specs=WHOLE, out_shape=out(*own.shape),
    )


def gram(pieces, trailing, tall, short, state, top=None):
    whole, _, _ = trailing
    width, columns = pieces[0][2].shape[1], whole.shape[1]
    rows = whole.shape[0]
    count, begins = len(pieces), state is None

    def kernel(whole_ref, high_ref, lower_ref, *refs):
        piece_refs, refs = refs[:count], refs[count:]
        total_of = None
        if not begins:
            total_of, refs = refs[2][...], refs[3:]
        held_ref, square_ref, total_ref, *refs = refs
        place = lax.axis_index("col")
        for (mask, offset, array), ref in zip(pieces, piece_refs):
            size = array.shape[0]
            block = place ^ mask
            upper = min(size, tall - offset)
            here = pl.ds(pl.multiple_of(block * tall + offset, math.gcd(tall, offset)), upper)
            vectors = jnp.concatenate(halves(ref[:upper, :]), 1)
            held_ref[here, :] = vectors
            term = narrow(vectors, high_ref[here, :], ROWS) + narrow(vectors, lower_ref[here, :], ROWS)
            term = term[:width] + term[width:]
            total_of = term if total_of is None else total_of + term
            if upper < size:
                there = pl.ds(pl.multiple_of(block * short, short), short)
                square_ref[there, :] = ref[upper:, :]
        total_ref[...] = total_of
        if top is not None:
            leading(0, top, whole_ref, held_ref, square_ref, total_of, None, *refs)

    arrays = [piece[2] for piece in pieces]
    taken = sum(array.shape[0] for array in arrays)
    states = () if begins else state
    return kernel_call(
        kernel, (*trailing, *arrays, *states),
        8 * taken * width * columns, 8 * taken * width,
        in_specs=[WHOLE] * (3 + count + len(states)),
        out_specs=[WHOLE] * (3 if top is None else 5),
        out_shape=[pltpu.VMEM((rows, 2 * width), jnp.bfloat16), out(width, width), out(width, columns)]
        + ([] if top is None else [out(top, columns)] * 2),
        input_output_aliases={} if begins else {3 + count: 0, 4 + count: 1},
    )


def leading(low, high, whole_ref, held_ref, square_ref, total, before, weights_ref, top_ref):
    width = square_ref.shape[0]
    weights = product(square_ref[:high, low:high], total[:high], ROWS)
    weights_ref[...] = weights
    if before is not None:
        weights = jnp.concatenate([before, weights], 0)
    vectors = held_ref[low:high, :]
    top_ref[...] = whole_ref[low:high, :] - thrice(vectors[:, :high], vectors[:, width : width + high], *halves(weights))


def weigh(low, high, trailing, held, square, total, before):
    columns = trailing.shape[1]

    def kernel(whole_ref, held_ref, square_ref, total_ref, before_ref, weights_ref, top_ref):
        leading(low, high, whole_ref, held_ref, square_ref, total_ref[...], before_ref[...], weights_ref, top_ref)

    return kernel_call(
        kernel, (trailing, held, square, total, before), 6 * high * high * columns, 8 * high * columns,
        in_specs=[WHOLE] * 5, out_specs=[WHOLE] * 2, out_shape=[out(high - low, columns)] * 2,
    )


def update(trailing, held, weights):
    rows, columns = trailing.shape
    panel = held.shape[1] // 2
    below = rows - panel
    tile = below // TILES if below % (16 * TILES) == 0 else panel
    tiles = below // tile
    chunks = len(weights)

    def kernel(trailing_ref, held_ref, *refs):
        weights_refs, (out_ref, result, factors, sems) = refs[:chunks], refs[chunks:]
        high, low = halves(jnp.concatenate([ref[...] for ref in weights_refs], 0))
        factors[:, :columns] = high
        factors[:, columns:] = low

        def rows_of(n):
            return pl.ds(pl.multiple_of(panel + n * tile, math.gcd(panel, tile)), tile)

        def store(n):
            return pltpu.make_async_copy(result.at[n], out_ref.at[rows_of(n)], sems.at[n])

        @pl.loop(0, tiles)
        def _(n):
            here = rows_of(n)
            both = narrow(held_ref[here, :panel], factors[...], PLAIN)
            rest = narrow(held_ref[here, panel:], factors[:, :columns], PLAIN)
            result[n] = trailing_ref[here, :] - (both[:, :columns] + (both[:, columns:] + rest))
            store(n).start()

        @pl.loop(0, tiles)
        def _(n):
            store(n).wait()

    return kernel_call(
        kernel, (trailing, held, *weights), 6 * rows * panel * columns, 4 * rows * columns, 4 * rows * columns + GRANT,
        in_specs=[WHOLE] * (2 + chunks), out_specs=HBM, out_shape=outside(rows, columns),
        scratch_shapes=[
            pltpu.VMEM((tiles, tile, columns), jnp.float32),
            pltpu.VMEM((panel, 2 * columns), jnp.bfloat16),
            pltpu.SemaphoreType.DMA((tiles,)),
        ],
    )


def combine(level, current, received, pair, order, full=False, settled=None, updated=None):
    columns = current[0].shape[1]
    count, covered = len(current), sum(array.shape[0] for array in current)
    width = current[-1].shape[0]
    panel = pair[0].shape[1]
    last = updated is not None

    def kernel(*refs):
        current_refs, received_refs, refs = refs[:count], refs[count : 2 * count], refs[2 * count :]
        pair_refs, refs = refs[: len(pair)], refs[len(pair) :]
        if settled is not None:
            settled_ref, *refs = refs
        if last:
            _, out_ref, vectors, factor, result, sem = refs
        elif full:
            result, chunk_ref, vectors, factor = refs
        else:
            chunk_ref, vectors, factor = refs
        short, half = panel // len(order), len(order) // 2
        for n, mask in enumerate(order):
            to = pl.multiple_of((lax.axis_index("col") ^ mask) * short, short)
            part, m = pair_refs[n // half], n % half
            vectors[pl.ds(to, short), :] = part[2 * m * short : (2 * m + 1) * short, :]
            factor[pl.ds(to, short), :] = part[(2 * m + 1) * short : (2 * m + 2) * short, :]
        role = role_of(level)
        mine = jnp.concatenate([ref[...] for ref in current_refs], 0)
        other = jnp.concatenate([ref[...] for ref in received_refs], 0)
        leads = role == 1
        lower, upper = jnp.where(leads, mine, other), jnp.where(leads, other, mine)
        both = lower + product(vectors[:covered, :covered], upper, ROWS)
        taken = factor[:covered, :covered] if full else factor[:covered, covered - width : covered]
        weights = product(taken, both, ROWS)
        if full:
            @pl.when(role == 0)
            def _():
                result[...] = mine if settled is None else settled_ref[...]

            @pl.when(role == 1)
            def _():
                result[...] = lower - weights

            @pl.when(role == 2)
            def _():
                result[...] = upper - product(vectors[...], weights, PLAIN)

        if not last:
            chunk_ref[...] = lower[covered - width :] - weights[weights.shape[0] - width :]
        else:
            store = pltpu.make_async_copy(result, out_ref.at[pl.ds(0, covered)], sem.at[0])
            store.start()
            store.wait()

    optional = tuple(array for array in (settled, updated) if array is not None)
    arguments = (*current, *received, *pair, *optional)
    chunk, every = out(width, columns), out(covered, columns)
    return kernel_call(
        kernel, arguments, 18 * covered * panel * columns, 16 * covered * columns,
        in_specs=[WHOLE] * (len(arguments) - last) + [HBM] * last,
        out_specs=HBM if last else [WHOLE] * 2 if full else WHOLE,
        out_shape=outside(*updated.shape) if last else [every, chunk] if full else chunk,
        scratch_shapes=[pltpu.VMEM((panel, panel), jnp.float32)] * 2
        + ([pltpu.VMEM((covered, columns), jnp.float32), pltpu.SemaphoreType.DMA((1,))] if last else []),
        input_output_aliases={len(arguments) - 1: 0} if last else {},
    )


def gathered(parts, bits):
    if len(parts) == 2:
        core, wide, high = bits
        far = wide ^ high
        (upper, lower), cut = parts, parts[0].shape[0]
        near_a, near_b = exchanged(upper, wide), exchanged(lower, high)
        rest_b, rest_a = exchanged(lower, wide), exchanged(upper, high)
        steps = [
            [(0, 0, upper), (0, cut, lower)],
            [(wide, 0, near_a), (high, cut, near_b)],
            [(wide, cut, rest_b), (high, 0, rest_a)],
            [(far, 0, exchanged(near_a, high)), (far, cut, exchanged(near_b, wide))],
        ]
        across = [[(mask ^ core, offset, exchanged(array, core)) for mask, offset, array in step] for step in steps]
        return [steps[0] + across[0], steps[1] + across[1], steps[2] + across[2], steps[3], across[3]]
    blocks = [(0, 0, parts[0])]
    steps = [blocks]
    for bit in reversed(bits):
        steps.append([(mask ^ bit, 0, exchanged(block, bit)) for mask, _, block in blocks])
        blocks = blocks + steps[-1]
    return steps


def doubled(array, masks):
    order = [0]
    for n, mask in enumerate(masks):
        arrays = [array, exchanged(array, mask)]
        order = order + [m ^ mask for m in order]
        if n < len(masks) - 1:
            array = join(arrays)
    return arrays, order


def shards(trailing, leaf_vectors, leaf_factor, tree_vectors, tree_factor):
    down, across = lax.axis_size("row"), lax.axis_size("col")
    levels = down.bit_length() - 1
    bits = [1 << n for n in range(across.bit_length() - 1)]
    panel = leaf_factor.shape[1]
    tall, short = leaf_vectors.shape[0], leaf_factor.shape[0]
    rows = tall + short
    ranges = [(0, tall // 2), (tall // 2, rows)] if len(bits) == 3 else [(0, rows)]
    *parts, own = pack(leaf_vectors, leaf_factor, tree_vectors, tree_factor, ranges)
    trailing = load(trailing)

    pairs = []
    for level in range(levels):
        stride = 1 << level
        sent = lax.ppermute(own, "row", [(k + stride, k) for k in range(0, down, 2 * stride)])
        pair, order = doubled(pick(level, own, sent), bits[1:] + bits[:1])
        pairs.append(pair)

    state = None
    steps = gathered(parts, bits)
    half = panel // 2
    for n, pieces in enumerate(steps):
        state = gram(pieces, trailing, tall, short, state, half if n == len(steps) - 1 else None)
    held, square, total, weights, top = state
    more_weights, more_top = weigh(half, panel, trailing[0], held, square, total, weights)
    updated = update(trailing[0], held, (weights, more_weights))
    tops = [top, more_top]
    current, settled = tops, None
    for level in range(levels):
        stride = 1 << level
        swap = [pair for k in range(0, down, 2 * stride) for pair in ((k + stride, k), (k + stride // 2, k + stride))]
        received = [lax.ppermute(array, "row", swap) for array in current]
        if level == levels - 1:
            return combine(level, current, received, pairs[level], order, True, settled, updated)
        ahead = [combine(level, current[: c + 1], received[: c + 1], pairs[level], order) for c in range(len(tops) - 1)]
        settled, chunk = combine(level, current, received, pairs[level], order, True, settled)
        current = ahead + [chunk]


def solution(mesh):
    placed = (
        P("row", "col"),
        P(("row", "col"), None),
        P(("row", "col"), None),
        P(("row", "col"), None),
        P(("row", "col"), None),
    )

    return jax.shard_map(shards, mesh=mesh, in_specs=placed, out_specs=P("row", "col"), check_vma=False)
```

```python
import math

import jax
import jax.numpy as jnp
from jax import lax
from jax.experimental import pallas as pl
from jax.experimental.pallas import tpu as pltpu
from jax.sharding import PartitionSpec as P


ROWS = (((0,), (0,)), ((), ()))
PLAIN = (((1,), (0,)), ((), ()))
HBM = pl.BlockSpec(memory_space=pltpu.HBM)
WHOLE = pl.BlockSpec(memory_space=pltpu.VMEM)
GRANT = 4 << 20
PARTS = 8
TILES = 6


def halves(array):
    high = array.astype(jnp.bfloat16)
    return high, (array - high.astype(jnp.float32)).astype(jnp.bfloat16)


def narrow(first, second, dims):
    return lax.dot_general(first, second, dims, preferred_element_type=jnp.float32)


def product(first, second, dims):
    first_high, first_low = halves(first)
    second_high, second_low = halves(second)
    return narrow(first_high, second_high, dims) + (
        narrow(first_high, second_low, dims) + narrow(first_low, second_high, dims)
    )


def thrice(high, low, factor_high, factor_low):
    return narrow(high, factor_high, PLAIN) + (narrow(high, factor_low, PLAIN) + narrow(low, factor_high, PLAIN))


def out(*shape):
    return pltpu.VMEM(shape, jnp.float32)


def outside(*shape):
    return pltpu.HBM(shape, jnp.float32)


def role_of(level):
    stride = 1 << level
    inside = lax.rem(lax.axis_index("row"), 2 * stride)
    return jnp.where(inside == 0, 1, jnp.where(inside == stride, 2, 0))


def outer(*arrays):
    return tuple(pltpu.with_memory_space_constraint(array, pltpu.HBM) for array in arrays)


def exchanged(array, mask):
    return lax.ppermute(array, "col", [(i, i ^ mask) for i in range(lax.axis_size("col"))])


def kernel_call(kernel, arguments, flops, moved, grant=GRANT, **options):
    return pl.pallas_call(
        kernel,
        compiler_params=pltpu.CompilerParams(vmem_limit_bytes=grant),
        cost_estimate=pl.CostEstimate(flops=flops, bytes_accessed=moved, transcendentals=0),
        **options,
    )(*arguments)


def pack(leaf_vectors, leaf_factor, tree_vectors, tree_factor, ranges):
    tall, short = leaf_vectors.shape[0], leaf_factor.shape[0]
    parts = len(ranges)

    def kernel(vectors_ref, factor_ref, tree_vectors_ref, tree_factor_ref, *refs):
        *part_refs, own_ref, sems = refs
        moves = [(tree_vectors_ref, own_ref.at[pl.ds(0, short)]), (tree_factor_ref, own_ref.at[pl.ds(short, short)])]
        for (start, stop), ref in zip(ranges, part_refs):
            upper = min(stop, tall) - start
            moves.append((vectors_ref.at[pl.ds(start, upper)], ref.at[pl.ds(0, upper)]))
            if stop > tall:
                moves.append((factor_ref, ref.at[pl.ds(upper, short)]))
        copies = [pltpu.make_async_copy(source, target, sems.at[n]) for n, (source, target) in enumerate(moves)]
        for copy in copies:
            copy.start()
        for copy in copies:
            copy.wait()

    width = leaf_vectors.shape[1]
    return kernel_call(
        kernel, outer(leaf_vectors, leaf_factor, tree_vectors, tree_factor), 0, 8 * tall * width,
        in_specs=[HBM] * 4, out_specs=[WHOLE] * (parts + 1),
        out_shape=[out(stop - start, width) for start, stop in ranges] + [out(2 * short, width)],
        scratch_shapes=[pltpu.SemaphoreType.DMA((parts + 3,))],
    )


def load(array):
    rows = array.shape[0] // PARTS

    def kernel(array_ref, out_ref, high_ref, low_ref, sems):
        copies = []
        for n in range(PARTS):
            part = pl.ds(n * rows, rows)
            copies.append(pltpu.make_async_copy(array_ref.at[part], out_ref.at[part], sems.at[n]))
            copies[-1].start()
        for n, copy in enumerate(copies):
            copy.wait()
            part = pl.ds(n * rows, rows)
            high_ref[part, :], low_ref[part, :] = halves(out_ref[part, :])

    shape = array.shape
    return kernel_call(
        kernel, outer(array), 0, 12 * array.size,
        in_specs=[HBM], out_specs=[WHOLE] * 3,
        out_shape=[out(*shape), pltpu.VMEM(shape, jnp.bfloat16), pltpu.VMEM(shape, jnp.bfloat16)],
        scratch_shapes=[pltpu.SemaphoreType.DMA((PARTS,))],
    )


def join(arrays):
    def kernel(*refs):
        start = 0
        for ref in refs[:-1]:
            refs[-1][start : start + ref.shape[0], :] = ref[...]
            start += ref.shape[0]

    rows = sum(array.shape[0] for array in arrays)
    return kernel_call(
        kernel, arrays, 0, 8 * rows * arrays[0].shape[1],
        in_specs=[WHOLE] * len(arrays), out_specs=WHOLE, out_shape=out(rows, arrays[0].shape[1]),
    )


def pick(level, own, sent):
    def kernel(own_ref, sent_ref, out_ref):
        out_ref[...] = jnp.where(role_of(level) == 2, own_ref[...], sent_ref[...])

    return kernel_call(
        kernel, (own, sent), 0, 12 * own.size,
        in_specs=[WHOLE, WHOLE], out_specs=WHOLE, out_shape=out(*own.shape),
    )


def gram(pieces, trailing, tall, short, state, part, span=None, before=None):
    whole, _, _ = trailing
    width, columns = pieces[0][2].shape[1], whole.shape[1]
    rows = whole.shape[0]
    count, begins = len(pieces), state is None
    first, last = part

    def kernel(whole_ref, high_ref, lower_ref, *refs):
        piece_refs, refs = refs[:count], refs[count:]
        total_of = None
        if not begins:
            total_of, refs = refs[2][first:last, :], refs[3:]
        if before is not None:
            before_ref, *refs = refs
        held_ref, square_ref, total_ref, *refs = refs
        place = lax.axis_index("col")
        for (mask, offset, array), ref in zip(pieces, piece_refs):
            size = array.shape[0]
            block = place ^ mask
            upper = min(size, tall - offset)
            here = pl.ds(pl.multiple_of(block * tall + offset, math.gcd(tall, offset)), upper)
            leads, trails = halves(ref[:upper, first:last])
            held_ref[here, first:last] = leads
            held_ref[here, width + first : width + last] = trails
            vectors = jnp.concatenate([leads, trails], 1)
            term = narrow(vectors, high_ref[here, :], ROWS) + narrow(vectors, lower_ref[here, :], ROWS)
            term = term[: last - first] + term[last - first :]
            total_of = term if total_of is None else total_of + term
            if upper < size:
                there = pl.ds(pl.multiple_of(block * short, short), short)
                square_ref[there, first:last] = ref[upper:, first:last]
        total_ref[first:last, :] = total_of
        if span is not None:
            weights = None if before is None else before_ref[...]
            leading(*span, whole_ref, held_ref, square_ref, total_ref[: span[1], :], weights, *refs)

    arrays = [piece[2] for piece in pieces]
    taken = sum(array.shape[0] for array in arrays)
    states = () if begins else state
    extra = () if before is None else (before,)
    return kernel_call(
        kernel, (*trailing, *arrays, *states, *extra),
        8 * taken * (last - first) * columns, 8 * taken * (last - first),
        in_specs=[WHOLE] * (3 + count + len(states) + len(extra)),
        out_specs=[WHOLE] * (3 if span is None else 5),
        out_shape=[pltpu.VMEM((rows, 2 * width), jnp.bfloat16), out(width, width), out(width, columns)]
        + ([] if span is None else [out(span[1] - span[0], columns)] * 2),
        input_output_aliases={} if begins else {3 + count + n: n for n in range(3)},
    )


def leading(low, high, whole_ref, held_ref, square_ref, total, before, weights_ref, top_ref):
    width = square_ref.shape[0]
    weights = product(square_ref[:high, low:high], total[:high], ROWS)
    weights_ref[...] = weights
    if before is not None:
        weights = jnp.concatenate([before, weights], 0)
    vectors = held_ref[low:high, :]
    top_ref[...] = whole_ref[low:high, :] - thrice(vectors[:, :high], vectors[:, width : width + high], *halves(weights))


def update(trailing, held, weights):
    rows, columns = trailing.shape
    panel = held.shape[1] // 2
    below = rows - panel
    tile = below // TILES if below % (16 * TILES) == 0 else panel
    tiles = below // tile
    chunks = len(weights)

    def kernel(trailing_ref, held_ref, *refs):
        weights_refs, (out_ref, result, factors, sems) = refs[:chunks], refs[chunks:]
        high, low = halves(jnp.concatenate([ref[...] for ref in weights_refs], 0))
        factors[:, :columns] = high
        factors[:, columns:] = low

        def rows_of(n):
            return pl.ds(pl.multiple_of(panel + n * tile, math.gcd(panel, tile)), tile)

        def store(n):
            return pltpu.make_async_copy(result.at[n], out_ref.at[rows_of(n)], sems.at[n])

        @pl.loop(0, tiles)
        def _(n):
            here = rows_of(n)
            both = narrow(held_ref[here, :panel], factors[...], PLAIN)
            rest = narrow(held_ref[here, panel:], factors[:, :columns], PLAIN)
            result[n] = trailing_ref[here, :] - (both[:, :columns] + (both[:, columns:] + rest))
            store(n).start()

        @pl.loop(0, tiles)
        def _(n):
            store(n).wait()

    return kernel_call(
        kernel, (trailing, held, *weights), 6 * rows * panel * columns, 4 * rows * columns, 4 * rows * columns + GRANT,
        in_specs=[WHOLE] * (2 + chunks), out_specs=HBM, out_shape=outside(rows, columns),
        scratch_shapes=[
            pltpu.VMEM((tiles, tile, columns), jnp.float32),
            pltpu.VMEM((panel, 2 * columns), jnp.bfloat16),
            pltpu.SemaphoreType.DMA((tiles,)),
        ],
    )


def combine(level, current, received, pair, order, full=False, settled=None, updated=None):
    columns = current[0].shape[1]
    count, covered = len(current), sum(array.shape[0] for array in current)
    width = current[-1].shape[0]
    panel = pair[0].shape[1]
    last = updated is not None

    def kernel(*refs):
        current_refs, received_refs, refs = refs[:count], refs[count : 2 * count], refs[2 * count :]
        pair_refs, refs = refs[: len(pair)], refs[len(pair) :]
        if settled is not None:
            settled_ref, *refs = refs
        if last:
            _, out_ref, vectors, factor, result, sem = refs
        elif full:
            result, chunk_ref, vectors, factor = refs
        else:
            chunk_ref, vectors, factor = refs
        short, half = panel // len(order), len(order) // 2
        for n, mask in enumerate(order):
            to = pl.multiple_of((lax.axis_index("col") ^ mask) * short, short)
            part, m = pair_refs[n // half], n % half
            vectors[pl.ds(to, short), :] = part[2 * m * short : (2 * m + 1) * short, :]
            factor[pl.ds(to, short), :] = part[(2 * m + 1) * short : (2 * m + 2) * short, :]
        role = role_of(level)
        mine = jnp.concatenate([ref[...] for ref in current_refs], 0)
        other = jnp.concatenate([ref[...] for ref in received_refs], 0)
        leads = role == 1
        lower, upper = jnp.where(leads, mine, other), jnp.where(leads, other, mine)
        both = lower + product(vectors[:covered, :covered], upper, ROWS)
        taken = factor[:covered, :covered] if full else factor[:covered, covered - width : covered]
        weights = product(taken, both, ROWS)
        if full:
            @pl.when(role == 0)
            def _():
                result[...] = mine if settled is None else settled_ref[...]

            @pl.when(role == 1)
            def _():
                result[...] = lower - weights

            @pl.when(role == 2)
            def _():
                result[...] = upper - product(vectors[...], weights, PLAIN)

        if not last:
            chunk_ref[...] = lower[covered - width :] - weights[weights.shape[0] - width :]
        else:
            store = pltpu.make_async_copy(result, out_ref.at[pl.ds(0, covered)], sem.at[0])
            store.start()
            store.wait()

    optional = tuple(array for array in (settled, updated) if array is not None)
    arguments = (*current, *received, *pair, *optional)
    chunk, every = out(width, columns), out(covered, columns)
    return kernel_call(
        kernel, arguments, 18 * covered * panel * columns, 16 * covered * columns,
        in_specs=[WHOLE] * (len(arguments) - last) + [HBM] * last,
        out_specs=HBM if last else [WHOLE] * 2 if full else WHOLE,
        out_shape=outside(*updated.shape) if last else [every, chunk] if full else chunk,
        scratch_shapes=[pltpu.VMEM((panel, panel), jnp.float32)] * 2
        + ([pltpu.VMEM((covered, columns), jnp.float32), pltpu.SemaphoreType.DMA((1,))] if last else []),
        input_output_aliases={len(arguments) - 1: 0} if last else {},
    )


def gathered(parts, bits):
    if len(parts) == 2:
        core, wide, high = bits
        far = wide ^ high
        (upper, lower), cut = parts, parts[0].shape[0]
        near_a, near_b = exchanged(upper, wide), exchanged(lower, high)
        rest_b, rest_a = exchanged(lower, wide), exchanged(upper, high)
        steps = [
            [(0, 0, upper), (0, cut, lower)],
            [(wide, 0, near_a), (high, cut, near_b)],
            [(wide, cut, rest_b), (high, 0, rest_a)],
            [(far, 0, exchanged(near_a, high)), (far, cut, exchanged(near_b, wide))],
        ]
        across = [[(mask ^ core, offset, exchanged(array, core)) for mask, offset, array in step] for step in steps]
        return [steps[0] + across[0], steps[1] + across[1], steps[2] + across[2], steps[3], across[3]]
    blocks = [(0, 0, parts[0])]
    steps = [blocks]
    for bit in reversed(bits):
        steps.append([(mask ^ bit, 0, exchanged(block, bit)) for mask, _, block in blocks])
        blocks = blocks + steps[-1]
    return steps


def doubled(array, masks):
    order = [0]
    for n, mask in enumerate(masks):
        arrays = [array, exchanged(array, mask)]
        order = order + [m ^ mask for m in order]
        if n < len(masks) - 1:
            array = join(arrays)
    return arrays, order


def shards(trailing, leaf_vectors, leaf_factor, tree_vectors, tree_factor):
    down, across = lax.axis_size("row"), lax.axis_size("col")
    levels = down.bit_length() - 1
    bits = [1 << n for n in range(across.bit_length() - 1)]
    panel = leaf_factor.shape[1]
    tall, short = leaf_vectors.shape[0], leaf_factor.shape[0]
    rows = tall + short
    ranges = [(0, tall // 2), (tall // 2, rows)] if len(bits) == 3 else [(0, rows)]
    *parts, own = pack(leaf_vectors, leaf_factor, tree_vectors, tree_factor, ranges)
    trailing = load(trailing)

    pairs = []
    for level in range(levels):
        stride = 1 << level
        sent = lax.ppermute(own, "row", [(k + stride, k) for k in range(0, down, 2 * stride)])
        pair, order = doubled(pick(level, own, sent), bits[1:] + bits[:1])
        pairs.append(pair)

    state = None
    steps = gathered(parts, bits)
    half = panel // 2
    left, right = (0, half), (half, panel)
    for pieces in steps[:-1]:
        state = gram(pieces, trailing, tall, short, state, (0, panel))
    *state, weights, top = gram(steps[-1], trailing, tall, short, state, left, left)
    *state, more_weights, more_top = gram(steps[-1], trailing, tall, short, state, right, right, weights)
    held = state[0]
    updated = update(trailing[0], held, (weights, more_weights))
    tops = [top, more_top]
    current, settled = tops, None
    for level in range(levels):
        stride = 1 << level
        swap = [pair for k in range(0, down, 2 * stride) for pair in ((k + stride, k), (k + stride // 2, k + stride))]
        received = [lax.ppermute(array, "row", swap) for array in current]
        if level == levels - 1:
            return combine(level, current, received, pairs[level], order, True, settled, updated)
        ahead = [combine(level, current[: c + 1], received[: c + 1], pairs[level], order) for c in range(len(tops) - 1)]
        settled, chunk = combine(level, current, received, pairs[level], order, True, settled)
        current = ahead + [chunk]


def solution(mesh):
    placed = (
        P("row", "col"),
        P(("row", "col"), None),
        P(("row", "col"), None),
        P(("row", "col"), None),
        P(("row", "col"), None),
    )

    return jax.shard_map(shards, mesh=mesh, in_specs=placed, out_specs=P("row", "col"), check_vma=False)
```
